256 devices in a mesh: samp: 64 (over z_lo, x, y, core), var: 4 (over z_hi).
Axes of the slice: x: 4, y: 4, z: 8 (z_hi: 4, z_lo: 2; z = z_hi * 2 + z_lo), core: 2. Of those that a mesh axis runs over, the one named last changes fastest.
Arguments:
- genotypes: bfloat16 [65536, 16384], P('samp', 'var'), may hold values from 0 to 2, as said below
- col_mean: float32 [16384], P('var'), may hold values from 0.1 to 1, as said below
- inv_scale: float32 [16384], P('var'), may hold values from 1.4 to 3.25, as said below
- targets: float32 [65536], P('samp'), may hold values from -6 to 6
- probes: float32 [65536, 7], P('samp'), may hold values from -6 to 6
- delta: float32 [1], replicated, may hold values from 0.5 to 2
Outputs:
- solution: float32 [65536, 8], P('samp')
- assoc: float32 [16384], P('var')
The draws below stay inside these ranges and needn't reach their ends.
Inputs may be any that keep to these rules, and one draw needn't show every extreme that they name: `genotypes`: dosages 0, 1 or 2, drawn per variant from an allele frequency f of 0.05 to 0.5. `col_mean`: 2 f for the variant's allele frequency f. `inv_scale`: 1 / sqrt(2 f (1 - f)) for the same frequency f.
All inputs are finite; a program needn't handle non-finite values.
Results may differ from the reference program's by a relative error of at most 0.0003.
Values sent between devices are 32-bit elements; how exact they have to be, the bound alone decides.
A program may use at most 64 MiB of HBM per device.

```python
import math
import jax
import jax.numpy as jnp
from jax import lax

M = 16384
COLS = 8
ITERS = 2
N = 65536


def allele_level(key):
    return jax.random.randint(jax.random.fold_in(key, 11), (M,), 50, 500)


def allele_freq(key):
    return allele_level(key).astype(jnp.float32) / 1000.0


def draw_genotypes(key, part):
    level = allele_level(key)
    values = jax.random.randint(jax.random.fold_in(key, 21), (N, M), 0, 1000000)
    first = (values % 1000 < level[None, :]).astype(jnp.float32)
    second = (values // 1000 < level[None, :]).astype(jnp.float32)
    return (first + second).astype(jnp.bfloat16)


def draw_col_mean(key, part):
    return 2.0 * allele_freq(key)


def draw_inv_scale(key, part):
    freq = allele_freq(key)
    return 1.0 / jnp.sqrt(2.0 * freq * (1.0 - freq))


def level_of(stream_key, shape, cuts, smallest, top_value):
    level = 1.0
    for axis_at, parts in cuts:
        steps = jax.random.uniform(jax.random.fold_in(jax.random.fold_in(stream_key, 6), axis_at), (parts,), jnp.float32, smallest / len(cuts), top_value / len(cuts))
        level = level * jnp.repeat(jnp.exp(steps), shape[axis_at] // parts).reshape((-1,) + (1,) * (len(shape) - 1 - axis_at))
    return level


def bell_draw(key, dims, width, reach, cuts=(), held_as=jnp.bfloat16):
    entries = width * jax.random.normal(key, dims, jnp.float32)
    if cuts:
        entries = entries * level_of(key, dims, cuts, -0.22, 0.18)
    return jnp.clip(entries, -reach, reach).astype(held_as)


def setup_inputs(seed: int = 0) -> dict:
    splits = jax.random.split(jax.random.key(seed), 7)
    genotypes = draw_genotypes(jax.random.fold_in(splits[6], 71), 0)
    col_mean = draw_col_mean(jax.random.fold_in(splits[6], 71), 0)
    inv_scale = draw_inv_scale(jax.random.fold_in(splits[6], 71), 0)
    targets = bell_draw(splits[3], (N,), 1.0, 6.0, ((0, 64),), jnp.float32)
    probes = bell_draw(splits[4], (N, COLS - 1), 1.0, 6.0, ((0, 64),), jnp.float32)
    delta = jnp.clip(jax.random.uniform(splits[5], (1,), jnp.float32, 0.5, 2.0), 0.5, 2.0)
    return {"genotypes": genotypes, "col_mean": col_mean, "inv_scale": inv_scale, "targets": targets, "probes": probes, "delta": delta}


HI = lax.Precision.HIGHEST

def blocks_of(genotypes):
    block = math.gcd(genotypes.shape[0], 512)
    return (genotypes.reshape(genotypes.shape[0] // block, block, genotypes.shape[1]), block)

def across(genotypes, col_mean, inv_scale, vectors):
    stacked, block = blocks_of(genotypes)
    pieces = vectors.reshape(stacked.shape[0], block, vectors.shape[1])

    def add_block(total, items):
        dense = items[0].astype(jnp.float32)
        return (total + lax.dot_general(dense, items[1], (((0,), (0,)), ((), ())), precision=HI, preferred_element_type=jnp.float32), None)
    start = jnp.zeros((genotypes.shape[1], vectors.shape[1]), jnp.float32)
    part, _ = lax.scan(add_block, start, (stacked, pieces))
    totals = lax.optimization_barrier(jnp.sum(vectors, 0))
    return inv_scale[:, None] * (part - col_mean[:, None] * totals[None, :])

def along(genotypes, col_mean, inv_scale, columns):
    stacked, block = blocks_of(genotypes)
    scaled = inv_scale[:, None] * columns
    offset = jnp.dot(col_mean, scaled, precision=HI, preferred_element_type=jnp.float32)
    rows = lax.map(lambda piece: jnp.dot(piece.astype(jnp.float32), scaled, precision=HI, preferred_element_type=jnp.float32), stacked)
    return rows.reshape(genotypes.shape[0], columns.shape[1]) - offset[None, :]

def reference(genotypes, col_mean, inv_scale, targets, probes, delta):
    shift = delta[0]
    rhs = jnp.concatenate([targets[:, None], probes], 1)
    solution = jnp.zeros_like(rhs)
    residual = rhs
    direction = rhs
    norm_now = lax.optimization_barrier(jnp.sum(residual * residual, 0))
    for step in range(ITERS):
        columns = across(genotypes, col_mean, inv_scale, direction)
        image = along(genotypes, col_mean, inv_scale, columns) / M + shift * direction
        alpha = norm_now / lax.optimization_barrier(jnp.sum(direction * image, 0))
        solution = solution + alpha[None, :] * direction
        residual = residual - alpha[None, :] * image
        norm_next = lax.optimization_barrier(jnp.sum(residual * residual, 0))
        direction = residual + (norm_next / norm_now)[None, :] * direction
        norm_now = norm_next
    first = across(genotypes, col_mean, inv_scale, solution[:, 0:1])[:, 0]
    assoc = first / jnp.sqrt(jnp.float32(N))
    return (solution, assoc)
```

```python
import functools
import math

import jax
import jax.numpy as jnp
from jax import lax
from jax.experimental import pallas as pl
from jax.experimental.pallas import tpu as pltpu
from jax.sharding import PartitionSpec as P

MESH = pl.DeviceIdType.MESH
PLACES = (2, 4, 4, 2)
COLS = 8
LANES = 128


def far(a, n):
    if n == 4:
        return lax.rem(2 + 3 * a + 3 * ((a * (a - 1)) // 2), 4)
    return n - 1 - a


def three(v):
    high = v.astype(jnp.bfloat16).astype(jnp.float32)
    rest = v - high
    mid = rest.astype(jnp.bfloat16).astype(jnp.float32)
    low = rest - mid
    return jnp.concatenate([high, mid, low], 0).astype(jnp.bfloat16)


def folded(p):
    return p[0:COLS] + p[COLS : 2 * COLS] + p[2 * COLS : 3 * COLS]


def kernel(
    places, n_var, n_total, m_total,
    g_hbm, mean_ref, inv_ref, target_ref, probe_ref, delta_ref,
    sol_ref, assoc_ref,
    g_ref, rhs_ref, send1, recv1, c0_ref, part_ref, send2, recv2, sums_ref, z_ref,
    g_sem, rs_send, rs_recv, ag_send, ag_recv, var_sem, sum_send, sum_recv, z_sem,
):
    n_zl, n_x, n_y, n_core = places
    n_samp = n_zl * n_x * n_y * n_core
    plane = n_x * n_y * n_core
    members = n_y * n_core
    half = COLS // n_core
    width = n_y * LANES
    n_z = n_var * n_zl
    me = lax.axis_index("samp")
    va = lax.axis_index("var")
    core = lax.rem(me, n_core)
    y = lax.rem(me // n_core, n_y)
    x = lax.rem(me // members, n_x)
    zl = me // plane
    z = va * n_zl + zl
    mine = me // members
    in_plane = lax.rem(me, plane)
    offsets = [(dz, dx) for dz in range(n_zl) for dx in range(n_x)]
    near_first = sorted(offsets, key=lambda o: (o[0] + min(o[1], n_x - o[1]), o))
    far_first = near_first[::-1]

    def group_of(o):
        return lax.rem(zl + o[0], n_zl) * n_x + lax.rem(x + o[1], n_x)

    def each_member(o, act):
        group = group_of(o)

        def one(k, carry):
            ty = lax.rem(y + far(k // n_core, n_y), n_y)
            tc = lax.rem(core + n_core - 1 - lax.rem(k, n_core), n_core)
            act(group * members + ty * n_core + tc)
            return carry

        lax.fori_loop(0, members - (1 if o == (0, 0) else 0), one, 0)

    def to(src, dst, send, recv, samp, var):
        pltpu.make_async_remote_copy(
            src_ref=src, dst_ref=dst, send_sem=send, recv_sem=recv, device_id=(samp, var), device_id_type=MESH
        ).start()

    def arrived(ref, count, sem):
        some = ref.at[pl.ds(0, count)]
        pltpu.make_async_copy(some, some, sem).wait()

    def block(i, group):
        columns = pl.ds(pl.multiple_of(group * width, width), width)
        return pltpu.make_async_copy(g_hbm.at[:, columns], g_ref.at[group], g_sem.at[i])

    for i, o in enumerate(far_first):
        block(i, group_of(o)).start()

    barrier = pltpu.get_barrier_semaphore()

    def greet(k, carry):
        pl.semaphore_signal(barrier, inc=1, device_id=(lax.rem(me + k, n_samp), va), device_id_type=MESH)
        return carry

    lax.fori_loop(1, n_samp, greet, 0)

    def on_line(d):
        tz = lax.rem(z + d, n_z)
        return lax.rem(tz, n_zl) * plane + in_plane, tz // n_zl

    for d in range(1, n_z):
        pl.semaphore_signal(barrier, inc=1, device_id=on_line(d), device_id_type=MESH)

    rhs_ref[0:1, :] = target_ref[...]
    rhs_ref[1:COLS, :] = probe_ref[...]
    rhs = rhs_ref[...]

    def reduced(vec, send, recv, sem, first):
        pieces = three(vec)
        total = jnp.sum(vec, 1, keepdims=True)
        before = None
        for i, o in enumerate(far_first):
            group = group_of(o)
            if first:
                block(i, group).wait()
            p = folded(jnp.dot(pieces, g_ref[group], preferred_element_type=jnp.float32))
            p = p - total * mean_ref[group]
            for ky in range(n_y):
                for kc in range(n_core):
                    send[group * members + ky * n_core + kc] = p[
                        kc * half : (kc + 1) * half, ky * LANES : (ky + 1) * LANES
                    ]
            if first and i == 0:
                pl.semaphore_wait(barrier, n_samp - 1 + n_z - 1)
            if before is not None:
                each_member(
                    before, lambda t: to(send.at[t], recv.at[me], rs_send.at[sem], rs_recv.at[sem], t, va)
                )
            before = o
        each_member(before, lambda t: to(send.at[t], recv.at[me], rs_send.at[sem], rs_recv.at[sem], t, va))
        recv[me] = send[me]
        arrived(recv, n_samp - 1, rs_recv.at[sem])
        scale = inv_ref[mine, :, pl.ds(pl.multiple_of(y * LANES, LANES), LANES)]
        return jnp.sum(recv[...], 0) * scale

    share0 = reduced(rhs, send1, recv1, 0, True)
    c0_ref[me] = share0
    for o in far_first:
        each_member(o, lambda t: to(c0_ref.at[me], c0_ref.at[me], ag_send, ag_recv.at[mine], t, va))

    rows = None
    shift = None
    for o in near_first:
        group = group_of(o)
        arrived(c0_ref, members - (1 if o == (0, 0) else 0), ag_recv.at[group])
        blocks = []
        for ky in range(n_y):
            blocks.append(
                jnp.concatenate([c0_ref[group * members + ky * n_core + kc] for kc in range(n_core)], 0)
            )
        scaled = jnp.concatenate(blocks, 1) * inv_ref[group]
        off = jnp.sum(scaled * mean_ref[group], 1, keepdims=True)
        p = lax.dot_general(
            three(scaled), g_ref[group], (((1,), (1,)), ((), ())), preferred_element_type=jnp.float32
        )
        rows = p if rows is None else rows + p
        shift = off if shift is None else shift + off
    part_ref[va] = folded(rows) - shift
    for d in sorted(range(1, n_var), key=lambda d: -min(d, n_var - d)):
        to(part_ref.at[va], part_ref.at[va], var_sem.at[0], var_sem.at[1], me, lax.rem(va + d, n_var))
    arrived(part_ref, n_var - 1, var_sem.at[1])
    image = part_ref[0]
    for k in range(1, n_var):
        image = image + part_ref[k]
    image = image * (1.0 / m_total)

    share1 = reduced(image, send2, recv2, 1, False)

    row = lax.broadcasted_iota(jnp.int32, (COLS, LANES), 0)
    lane = lax.broadcasted_iota(jnp.int32, (COLS, LANES), 1)
    own = row // half == core

    def by_column(a):
        spread = jnp.where(own, jnp.concatenate([a] * n_core, 0), 0.0)
        return jnp.sum(spread, 1, keepdims=True)

    def by_sample(a):
        return jnp.sum(a, 1, keepdims=True) * (1.0 / n_var)

    found = [
        by_column(share0 * share0), by_column(share0 * share1), by_column(share1 * share1),
        by_sample(rhs * rhs), by_sample(rhs * image), by_sample(image * image),
    ]
    spread = jnp.zeros((COLS, LANES), jnp.float32)
    for k, q in enumerate(found):
        spread = jnp.where(lane == row + COLS * k, q, spread)
    sums_ref[me] = jnp.concatenate([jnp.sum(spread, 0, keepdims=True), share1[0:1, :]], 0)
    for o in sorted(far_first, key=lambda o: o[0]):
        each_member(o, lambda t: to(sums_ref.at[me], sums_ref.at[me], sum_send, sum_recv.at[zl], t, va))
    arrived(sums_ref, plane - 1, sum_recv.at[zl])
    z_ref[z] = jnp.sum(sums_ref[pl.ds(zl * plane, plane)], 0)[0:1, :]
    for d in sorted(range(1, n_z), key=lambda d: -min(d, n_z - d)):
        to(z_ref.at[z], z_ref.at[z], z_sem.at[0], z_sem.at[1], *on_line(d))
    for other in range(1, n_zl):
        arrived(sums_ref, plane, sum_recv.at[lax.rem(zl + other, n_zl)])
    arrived(z_ref, n_z - 1, z_sem.at[1])
    every = jnp.broadcast_to(jnp.sum(z_ref[...], 0), (COLS, LANES))
    cc, cw, ww, rr, ri, ii = [
        jnp.sum(jnp.where(lane == row + COLS * k, every, 0.0), 1, keepdims=True) for k in range(len(found))
    ]

    delta = delta_ref[0]
    slope = ri / rr
    alpha0 = rr / (ri + delta * rr)
    norm1 = alpha0 * alpha0 * (ii - slope * ri)
    beta = norm1 / rr
    lead = alpha0 * slope + beta
    across = lead * lead * cc - 2.0 * lead * alpha0 * cw + alpha0 * alpha0 * ww
    alpha1 = norm1 / (across * (1.0 / m_total) + delta * (norm1 + beta * beta * rr))
    keep = alpha0 + alpha1 * lead
    less = alpha1 * alpha0
    sol_ref[...] = keep * rhs - less * image
    root = 1.0 / math.sqrt(n_total)
    keep_row = jnp.broadcast_to(keep[0:1, 0:1] * root, (1, LANES))
    less_row = jnp.broadcast_to(less[0:1, 0:1] * root, (1, LANES))
    for q in range(n_samp // n_core):
        at = q * n_core
        assoc_ref[q] = keep_row * c0_ref[at, 0:1, :] - less_row * sums_ref[at, 1:2, :]

    arrived(send1, n_samp - 1, rs_send.at[0])
    arrived(c0_ref, n_samp - 1, ag_send)
    arrived(part_ref, n_var - 1, var_sem.at[0])
    arrived(send2, n_samp - 1, rs_send.at[1])
    arrived(sums_ref, n_samp - 1, sum_send)
    arrived(z_ref, n_z - 1, z_sem.at[0])


def per_device(places, n_var, genotypes, col_mean, inv_scale, targets, probes, delta):
    n_zl, n_x, n_y, n_core = places
    n_samp = math.prod(places)
    n_loc, m_loc = genotypes.shape
    groups, width = n_zl * n_x, n_y * LANES
    n_z = n_var * n_zl
    f32 = jnp.float32
    vmem = pl.BlockSpec(memory_space=pltpu.VMEM)
    dma = pltpu.SemaphoreType.DMA
    sol, assoc = pl.pallas_call(
        functools.partial(kernel, places, n_var, n_loc * n_samp, m_loc * n_var),
        out_shape=(
            jax.ShapeDtypeStruct((COLS, n_loc), f32),
            jax.ShapeDtypeStruct((m_loc // LANES, 1, LANES), f32),
        ),
        in_specs=[pl.BlockSpec(memory_space=pl.ANY)] + [vmem] * 4 + [pl.BlockSpec(memory_space=pltpu.SMEM)],
        out_specs=(vmem, vmem),
        scratch_shapes=[
            pltpu.VMEM((groups, n_loc, width), jnp.bfloat16),
            pltpu.VMEM((COLS, n_loc), f32),
            pltpu.VMEM((n_samp, COLS // n_core, LANES), f32),
            pltpu.VMEM((n_samp, COLS // n_core, LANES), f32),
            pltpu.VMEM((n_samp, COLS // n_core, LANES), f32),
            pltpu.VMEM((n_var, COLS, n_loc), f32),
            pltpu.VMEM((n_samp, COLS // n_core, LANES), f32),
            pltpu.VMEM((n_samp, COLS // n_core, LANES), f32),
            pltpu.VMEM((n_samp, 2, LANES), f32),
            pltpu.VMEM((n_z, 1, LANES), f32),
            dma((groups,)),
            dma((2,)),
            dma((2,)),
            dma,
            dma((groups,)),
            dma((2,)),
            dma,
            dma((n_zl,)),
            dma((2,)),
        ],
        compiler_params=pltpu.CompilerParams(
            collective_id=0, has_side_effects=True, vmem_limit_bytes=60 * 1024 * 1024
        ),
    )(
        genotypes,
        col_mean.reshape(groups, 1, width),
        inv_scale.reshape(groups, 1, width),
        targets.reshape(1, n_loc),
        probes.T,
        delta,
    )
    return sol.T, assoc.reshape(m_loc)


def solution(mesh):
    places = PLACES
    if math.prod(places) != mesh.shape["samp"]:
        raise ValueError("samp size")
    placed = (P("samp", "var"), P("var"), P("var"), P("samp"), P("samp", None), P())
    return jax.shard_map(
        functools.partial(per_device, places, mesh.shape["var"]),
        mesh=mesh,
        in_specs=placed,
        out_specs=(P("samp", None), P("var")),
        check_vma=False,
    )
```

```python
import functools
import math

import jax
import jax.numpy as jnp
from jax import lax
from jax.experimental import pallas as pl
from jax.experimental.pallas import tpu as pltpu
from jax.sharding import PartitionSpec as P

MESH = pl.DeviceIdType.MESH
PLACES = (2, 4, 4, 2)
COLS = 8
LANES = 128
AHEAD = 3
HELD = 5


def apart(d, n):
    return min(d, n - d)


def three(v):
    high = v.astype(jnp.bfloat16).astype(jnp.float32)
    rest = v - high
    mid = rest.astype(jnp.bfloat16).astype(jnp.float32)
    low = rest - mid
    return jnp.concatenate([high, mid, low], 0).astype(jnp.bfloat16)


def folded(p):
    return p[0:COLS] + p[COLS : 2 * COLS] + p[2 * COLS : 3 * COLS]


def kernel(
    places, n_var, n_total, m_total,
    g_hbm, mean_hbm, inv_hbm, target_hbm, probe_hbm, delta_hbm,
    sol_hbm, assoc_hbm,
    g_ref, mean_ref, inv_ref, target_ref, probe_ref, delta_ref, sol_ref, assoc_ref,
    rhs_ref, send1, recv1, c0_ref, part_ref, send2, recv2, sums_ref, z_ref,
    g_sem, in_sem, out_sem, rs_send, rs_recv, ag_send, ag_recv, var_sem, sum_send, sum_recv, z_sem,
):
    n_zl, n_x, n_y, n_core = places
    n_samp = n_zl * n_x * n_y * n_core
    plane = n_x * n_y * n_core
    members = n_y * n_core
    half = COLS // n_core
    width = n_y * LANES
    n_z = n_var * n_zl
    me = lax.axis_index("samp")
    va = lax.axis_index("var")
    core = lax.rem(me, n_core)
    y = lax.rem(me // n_core, n_y)
    x = lax.rem(me // members, n_x)
    zl = me // plane
    z = va * n_zl + zl
    mine = me // members
    in_plane = lax.rem(me, plane)
    offsets = [(dz, dx) for dz in range(n_zl) for dx in range(n_x)]
    near_first = sorted(offsets, key=lambda o: (o[0] + apart(o[1], n_x), o))
    far_first = near_first[::-1]
    group_of = {o: lax.rem(zl + o[0], n_zl) * n_x + lax.rem(x + o[1], n_x) for o in offsets}
    steps = sorted(((dy, dc) for dy in range(n_y) for dc in range(n_core)), key=lambda m: (-apart(m[0], n_y), -m[1]))
    steps.remove((0, 0))
    member_of = [lax.rem(y + dy, n_y) * n_core + lax.rem(core + dc, n_core) for dy, dc in steps + [(0, 0)]]

    def each_member(o, act):
        first = group_of[o] * members
        for k in range(members - (1 if o == (0, 0) else 0)):
            act(first + member_of[k])

    def on_line(d):
        tz = lax.rem(z + d, n_z)
        return lax.rem(tz, n_zl) * plane + in_plane, tz // n_zl

    def to(src, dst, send, recv, samp, var):
        pltpu.make_async_remote_copy(
            src_ref=src, dst_ref=dst, send_sem=send, recv_sem=recv, device_id=(samp, var), device_id_type=MESH
        ).start()

    def arrived(ref, count, sem):
        some = ref.at[pl.ds(0, count)]
        pltpu.make_async_copy(some, some, sem).wait()

    def block(i, group):
        columns = pl.ds(pl.multiple_of(group * width, width), width)
        return pltpu.make_async_copy(g_hbm.at[:, columns], g_ref.at[group], g_sem.at[i])

    taken = [
        pltpu.make_async_copy(src, dst, in_sem.at[i])
        for i, (src, dst) in enumerate([
            (target_hbm, target_ref), (probe_hbm, probe_ref), (mean_hbm, mean_ref), (inv_hbm, inv_ref),
            (delta_hbm, delta_ref),
        ])
    ]
    for copy in taken:
        copy.start()
    for i in range(AHEAD):
        block(i, group_of[far_first[i]]).start()

    barrier = pltpu.get_barrier_semaphore()

    def greet(samp, var):
        pl.semaphore_signal(barrier, inc=1, device_id=(samp, var), device_id_type=MESH)

    for o in far_first:
        each_member(o, lambda t: greet(t, va))
    for d in range(1, n_z):
        greet(*on_line(d))

    for copy in taken:
        copy.wait()

    rhs_ref[0:1, :] = target_ref[...]
    rhs_ref[1:COLS, :] = probe_ref[...]
    rhs = rhs_ref[...]

    def reduced(vec, send, recv, sem, first, meanwhile):
        pieces = three(vec)
        total = jnp.sum(vec, 1, keepdims=True)

        def send_group(o):
            each_member(o, lambda t: to(send.at[t], recv.at[me], rs_send.at[sem], rs_recv.at[sem], t, va))

        for i, o in enumerate(far_first):
            group = group_of[o]
            if first:
                block(i, group).wait()
                if i + AHEAD < len(far_first):
                    block(i + AHEAD, group_of[far_first[i + AHEAD]]).start()
            p = folded(jnp.dot(pieces, g_ref[group], preferred_element_type=jnp.float32))
            p = p - total * mean_ref[group]
            held = min(HELD, len(far_first) - 1) if first else 1
            if first and i == held:
                pl.semaphore_wait(barrier, n_samp - 1 + n_z - 1)
            if i == held:
                for k in range(i):
                    send_group(far_first[k])
            elif i > held:
                send_group(far_first[i - 1])
            for ky in range(n_y):
                for kc in range(n_core):
                    send[group * members + ky * n_core + kc] = p[
                        kc * half : (kc + 1) * half, ky * LANES : (ky + 1) * LANES
                    ]
        send_group(far_first[-1])
        recv[me] = send[me]
        done = meanwhile()
        arrived(recv, n_samp - 1, rs_recv.at[sem])
        scale = inv_ref[mine, :, pl.ds(pl.multiple_of(y * LANES, LANES), LANES)]
        return jnp.sum(recv[...], 0) * scale, done

    share0, _ = reduced(rhs, send1, recv1, 0, True, lambda: None)
    c0_ref[me] = share0
    for o in far_first:
        each_member(o, lambda t: to(c0_ref.at[me], c0_ref.at[me], ag_send, ag_recv.at[mine], t, va))

    rows = None
    shift = None
    for o in near_first:
        group = group_of[o]
        arrived(c0_ref, members - (1 if o == (0, 0) else 0), ag_recv.at[group])
        blocks = []
        for ky in range(n_y):
            blocks.append(
                jnp.concatenate([c0_ref[group * members + ky * n_core + kc] for kc in range(n_core)], 0)
            )
        scaled = jnp.concatenate(blocks, 1) * inv_ref[group]
        off = jnp.sum(scaled * mean_ref[group], 1, keepdims=True)
        p = lax.dot_general(
            three(scaled), g_ref[group], (((1,), (1,)), ((), ())), preferred_element_type=jnp.float32
        )
        rows = p if rows is None else rows + p
        shift = off if shift is None else shift + off
    part_ref[va] = folded(rows) - shift
    for d in sorted(range(1, n_var), key=lambda d: -min(d, n_var - d)):
        to(part_ref.at[va], part_ref.at[va], var_sem.at[0], var_sem.at[1], me, lax.rem(va + d, n_var))
    arrived(part_ref, n_var - 1, var_sem.at[1])
    image = part_ref[0]
    for k in range(1, n_var):
        image = image + part_ref[k]
    image = image * (1.0 / m_total)

    row = lax.broadcasted_iota(jnp.int32, (COLS, LANES), 0)
    lane = lax.broadcasted_iota(jnp.int32, (COLS, LANES), 1)
    own = row // half == core

    def put(spread, k, q):
        return jnp.where(lane == row + COLS * k, jnp.sum(q, 1, keepdims=True), spread)

    def by_column(a):
        return jnp.where(own, jnp.concatenate([a] * n_core, 0), 0.0)

    def known():
        spread = put(jnp.zeros((COLS, LANES), jnp.float32), 0, by_column(share0 * share0))
        for k, (a, b) in enumerate([(rhs, rhs), (rhs, image), (image, image)]):
            spread = put(spread, 3 + k, a * b * (1.0 / n_var))
        return spread

    share1, spread = reduced(image, send2, recv2, 1, False, known)
    spread = put(spread, 1, by_column(share0 * share1))
    spread = put(spread, 2, by_column(share1 * share1))
    sums_ref[me] = jnp.concatenate([jnp.sum(spread, 0, keepdims=True), share1[0:1, :]], 0)
    for o in sorted(far_first, key=lambda o: o[0]):
        each_member(o, lambda t: to(sums_ref.at[me], sums_ref.at[me], sum_send, sum_recv.at[zl], t, va))
    arrived(sums_ref, plane - 1, sum_recv.at[zl])
    z_ref[z] = jnp.sum(sums_ref[pl.ds(zl * plane, plane)], 0)[0:1, :]
    for d in sorted(range(1, n_z), key=lambda d: -min(d, n_z - d)):
        to(z_ref.at[z], z_ref.at[z], z_sem.at[0], z_sem.at[1], *on_line(d))
    for other in range(1, n_zl):
        arrived(sums_ref, plane, sum_recv.at[lax.rem(zl + other, n_zl)])
    arrived(z_ref, n_z - 1, z_sem.at[1])
    every = jnp.broadcast_to(jnp.sum(z_ref[...], 0), (COLS, LANES))
    cc, cw, ww, rr, ri, ii = [
        jnp.sum(jnp.where(lane == row + COLS * k, every, 0.0), 1, keepdims=True) for k in range(6)
    ]

    delta = delta_ref[0]
    slope = ri / rr
    alpha0 = rr / (ri + delta * rr)
    norm1 = alpha0 * alpha0 * (ii - slope * ri)
    beta = norm1 / rr
    lead = alpha0 * slope + beta
    across = lead * lead * cc - 2.0 * lead * alpha0 * cw + alpha0 * alpha0 * ww
    alpha1 = norm1 / (across * (1.0 / m_total) + delta * (norm1 + beta * beta * rr))
    keep = alpha0 + alpha1 * lead
    less = alpha1 * alpha0
    sol_ref[...] = keep * rhs - less * image
    sol_out = pltpu.make_async_copy(sol_ref, sol_hbm, out_sem.at[0])
    sol_out.start()
    root = 1.0 / math.sqrt(n_total)
    keep_row = jnp.broadcast_to(keep[0:1, 0:1] * root, (1, LANES))
    less_row = jnp.broadcast_to(less[0:1, 0:1] * root, (1, LANES))
    for q in range(n_samp // n_core):
        at = q * n_core
        assoc_ref[q] = keep_row * c0_ref[at, 0:1, :] - less_row * sums_ref[at, 1:2, :]

    assoc_out = pltpu.make_async_copy(assoc_ref, assoc_hbm, out_sem.at[1])
    assoc_out.start()
    arrived(send1, n_samp - 1, rs_send.at[0])
    arrived(c0_ref, n_samp - 1, ag_send)
    arrived(part_ref, n_var - 1, var_sem.at[0])
    arrived(send2, n_samp - 1, rs_send.at[1])
    arrived(sums_ref, n_samp - 1, sum_send)
    arrived(z_ref, n_z - 1, z_sem.at[0])
    sol_out.wait()
    assoc_out.wait()


def per_device(places, n_var, genotypes, col_mean, inv_scale, targets, probes, delta):
    n_zl, n_x, n_y, n_core = places
    n_samp = math.prod(places)
    n_loc, m_loc = genotypes.shape
    groups, width = n_zl * n_x, n_y * LANES
    n_z = n_var * n_zl
    f32 = jnp.float32
    hbm = pl.BlockSpec(memory_space=pltpu.HBM)
    dma = pltpu.SemaphoreType.DMA
    sol, assoc = pl.pallas_call(
        functools.partial(kernel, places, n_var, n_loc * n_samp, m_loc * n_var),
        out_shape=(
            jax.ShapeDtypeStruct((COLS, n_loc), f32),
            jax.ShapeDtypeStruct((m_loc // LANES, 1, LANES), f32),
        ),
        in_specs=[hbm] * 6,
        out_specs=(hbm, hbm),
        scratch_shapes=[
            pltpu.VMEM((groups, n_loc, width), jnp.bfloat16),
            pltpu.VMEM((groups, 1, width), f32),
            pltpu.VMEM((groups, 1, width), f32),
            pltpu.VMEM((1, n_loc), f32),
            pltpu.VMEM((COLS - 1, n_loc), f32),
            pltpu.SMEM((1,), f32),
            pltpu.VMEM((COLS, n_loc), f32),
            pltpu.VMEM((m_loc // LANES, 1, LANES), f32),
            pltpu.VMEM((COLS, n_loc), f32),
            pltpu.VMEM((n_samp, COLS // n_core, LANES), f32),
            pltpu.VMEM((n_samp, COLS // n_core, LANES), f32),
            pltpu.VMEM((n_samp, COLS // n_core, LANES), f32),
            pltpu.VMEM((n_var, COLS, n_loc), f32),
            pltpu.VMEM((n_samp, COLS // n_core, LANES), f32),
            pltpu.VMEM((n_samp, COLS // n_core, LANES), f32),
            pltpu.VMEM((n_samp, 2, LANES), f32),
            pltpu.VMEM((n_z, 1, LANES), f32),
            dma((groups,)),
            dma((5,)),
            dma((2,)),
            dma((2,)),
            dma((2,)),
            dma,
            dma((groups,)),
            dma((2,)),
            dma,
            dma((n_zl,)),
            dma((2,)),
        ],
        compiler_params=pltpu.CompilerParams(
            collective_id=0, has_side_effects=True, vmem_limit_bytes=60 * 1024 * 1024
        ),
    )(
        genotypes,
        col_mean.reshape(groups, 1, width),
        inv_scale.reshape(groups, 1, width),
        targets.reshape(1, n_loc),
        probes.T,
        delta,
    )
    return sol.T, assoc.reshape(m_loc)


def solution(mesh):
    places = PLACES
    if math.prod(places) != mesh.shape["samp"]:
        raise ValueError("samp size")
    placed = (P("samp", "var"), P("var"), P("var"), P("samp"), P("samp", None), P())
    return jax.shard_map(
        functools.partial(per_device, places, mesh.shape["var"]),
        mesh=mesh,
        in_specs=placed,
        out_specs=(P("samp", None), P("var")),
        check_vma=False,
    )
```

```python
import functools
import math

import jax
import jax.numpy as jnp
from jax import lax
from jax.experimental import pallas as pl
from jax.experimental.pallas import tpu as pltpu
from jax.sharding import PartitionSpec as P

MESH = pl.DeviceIdType.MESH
PLACES = (2, 4, 4, 2)
COLS = 8
LANES = 128
AHEAD = 3
HELD = 5


def apart(d, n):
    return min(d, n - d)


def three(v):
    high = v.astype(jnp.bfloat16).astype(jnp.float32)
    rest = v - high
    mid = rest.astype(jnp.bfloat16).astype(jnp.float32)
    low = rest - mid
    return jnp.concatenate([high, mid, low], 0).astype(jnp.bfloat16)


def folded(p):
    return p[0:COLS] + p[COLS : 2 * COLS] + p[2 * COLS : 3 * COLS]


def kernel(
    places, n_var, n_total, m_total,
    g_hbm, mean_hbm, inv_hbm, target_hbm, probe_hbm, delta_hbm,
    sol_hbm, assoc_hbm,
    g_ref, mean_ref, inv_ref, target_ref, probe_ref, delta_ref, sol_ref, assoc_ref,
    rhs_ref, send1, recv1, c0_ref, part_ref, send2, recv2, sums_ref, own_ref, all_ref, z_ref,
    g_sem, in_sem, out_sem, rs_send, rs_recv, ag_send, ag_recv, var_sem, sum_send, sum_recv, all_send, all_recv,
):
    n_zl, n_x, n_y, n_core = places
    n_samp = n_zl * n_x * n_y * n_core
    plane = n_x * n_y * n_core
    members = n_y * n_core
    half = COLS // n_core
    width = n_y * LANES
    me = lax.axis_index("samp")
    va = lax.axis_index("var")
    core = lax.rem(me, n_core)
    y = lax.rem(me // n_core, n_y)
    x = lax.rem(me // members, n_x)
    zl = me // plane
    mine = me // members
    offsets = [(dz, dx) for dz in range(n_zl) for dx in range(n_x)]
    near_first = sorted(offsets, key=lambda o: (o[0] + apart(o[1], n_x), o))
    far_first = near_first[::-1]
    group_of = {o: lax.rem(zl + o[0], n_zl) * n_x + lax.rem(x + o[1], n_x) for o in offsets}
    steps = sorted(((dy, dc) for dy in range(n_y) for dc in range(n_core)), key=lambda m: (-apart(m[0], n_y), -m[1]))
    steps.remove((0, 0))
    member_of = [lax.rem(y + dy, n_y) * n_core + lax.rem(core + dc, n_core) for dy, dc in steps + [(0, 0)]]

    def each_member(o, act):
        first = group_of[o] * members
        for k in range(members - (1 if o == (0, 0) else 0)):
            act(first + member_of[k])

    def to(src, dst, send, recv, samp, var):
        pltpu.make_async_remote_copy(
            src_ref=src, dst_ref=dst, send_sem=send, recv_sem=recv, device_id=(samp, var), device_id_type=MESH
        ).start()

    def arrived(ref, count, sem):
        some = ref.at[pl.ds(0, count)]
        pltpu.make_async_copy(some, some, sem).wait()

    def block(i, group):
        columns = pl.ds(pl.multiple_of(group * width, width), width)
        return pltpu.make_async_copy(g_hbm.at[:, columns], g_ref.at[group], g_sem.at[i])

    taken = [
        pltpu.make_async_copy(src, dst, in_sem.at[i])
        for i, (src, dst) in enumerate([
            (target_hbm, target_ref), (probe_hbm, probe_ref), (mean_hbm, mean_ref), (inv_hbm, inv_ref),
            (delta_hbm, delta_ref),
        ])
    ]
    for copy in taken:
        copy.start()
    for i in range(AHEAD):
        block(i, group_of[far_first[i]]).start()

    barrier = pltpu.get_barrier_semaphore()

    def greet(samp, var):
        pl.semaphore_signal(barrier, inc=1, device_id=(samp, var), device_id_type=MESH)

    others = [(o, k, o[0] + apart(o[1], n_x) + apart(m[0], n_y)) for o in offsets for k, m in enumerate(steps)]
    others += [(o, members - 1, o[0] + apart(o[1], n_x)) for o in offsets if o != (0, 0)]
    peers = [(hops, group_of[o] * members + member_of[k], va) for o, k, hops in others]
    peers += [(n_zl * apart(d, n_var), me, lax.rem(va + d, n_var)) for d in range(1, n_var)]
    for _, samp, var in sorted(peers, key=lambda p: -p[0]):
        greet(samp, var)

    for copy in taken:
        copy.wait()

    rhs_ref[0:1, :] = target_ref[...]
    rhs_ref[1:COLS, :] = probe_ref[...]
    rhs = rhs_ref[...]

    def reduced(vec, send, recv, sem, first, meanwhile):
        pieces = three(vec)
        total = jnp.sum(vec, 1, keepdims=True)

        def send_group(o):
            each_member(o, lambda t: to(send.at[t], recv.at[me], rs_send.at[sem], rs_recv.at[sem], t, va))

        for i, o in enumerate(far_first):
            group = group_of[o]
            if first:
                block(i, group).wait()
                if i + AHEAD < len(far_first):
                    block(i + AHEAD, group_of[far_first[i + AHEAD]]).start()
            p = folded(jnp.dot(pieces, g_ref[group], preferred_element_type=jnp.float32))
            p = p - total * mean_ref[group]
            held = min(HELD, len(far_first) - 1) if first else 1
            if first and i == held:
                pl.semaphore_wait(barrier, n_samp - 1 + n_var - 1)
            if i == held:
                for k in range(i):
                    send_group(far_first[k])
            elif i > held:
                send_group(far_first[i - 1])
            for ky in range(n_y):
                for kc in range(n_core):
                    send[group * members + ky * n_core + kc] = p[
                        kc * half : (kc + 1) * half, ky * LANES : (ky + 1) * LANES
                    ]
        send_group(far_first[-1])
        recv[me] = send[me]
        done = meanwhile()
        arrived(recv, n_samp - 1, rs_recv.at[sem])
        scale = inv_ref[mine, :, pl.ds(pl.multiple_of(y * LANES, LANES), LANES)]
        return jnp.sum(recv[...], 0) * scale, done

    share0, _ = reduced(rhs, send1, recv1, 0, True, lambda: None)
    c0_ref[me] = share0
    for o in far_first:
        each_member(o, lambda t: to(c0_ref.at[me], c0_ref.at[me], ag_send, ag_recv.at[mine], t, va))

    rows = None
    shift = None
    rings = sorted({o[0] + apart(o[1], n_x) for o in offsets})
    stages = [[o for o in near_first if o[0] + apart(o[1], n_x) == r] for r in rings]
    for stage in stages:
        for o in stage:
            arrived(c0_ref, members - (1 if o == (0, 0) else 0), ag_recv.at[group_of[o]])
        for o in stage:
            group = group_of[o]
            blocks = []
            for ky in range(n_y):
                blocks.append(
                    jnp.concatenate([c0_ref[group * members + ky * n_core + kc] for kc in range(n_core)], 0)
                )
            scaled = jnp.concatenate(blocks, 1) * inv_ref[group]
            off = jnp.sum(scaled * mean_ref[group], 1, keepdims=True)
            p = lax.dot_general(
                three(scaled), g_ref[group], (((1,), (1,)), ((), ())), preferred_element_type=jnp.float32
            )
            rows = p if rows is None else rows + p
            shift = off if shift is None else shift + off
    part_ref[va] = folded(rows) - shift
    for d in sorted(range(1, n_var), key=lambda d: -min(d, n_var - d)):
        to(part_ref.at[va], part_ref.at[va], var_sem.at[0], var_sem.at[1], me, lax.rem(va + d, n_var))
    arrived(part_ref, n_var - 1, var_sem.at[1])
    image = part_ref[0]
    for k in range(1, n_var):
        image = image + part_ref[k]
    image = image * (1.0 / m_total)

    row = lax.broadcasted_iota(jnp.int32, (COLS, LANES), 0)
    lane = lax.broadcasted_iota(jnp.int32, (COLS, LANES), 1)
    own = row // half == core

    def put(spread, k, q):
        return jnp.where(lane == row + COLS * k, jnp.sum(q, 1, keepdims=True), spread)

    def by_column(a):
        return jnp.where(own, jnp.concatenate([a] * n_core, 0), 0.0)

    def known():
        spread = put(jnp.zeros((COLS, LANES), jnp.float32), 0, by_column(share0 * share0))
        for k, (a, b) in enumerate([(rhs, rhs), (rhs, image), (image, image)]):
            spread = put(spread, 3 + k, a * b * (1.0 / n_var))
        return spread

    share1, spread = reduced(image, send2, recv2, 1, False, known)
    spread = put(spread, 1, by_column(share0 * share1))
    spread = put(spread, 2, by_column(share1 * share1))
    sums_ref[me] = jnp.concatenate([jnp.sum(spread, 0, keepdims=True), share1[0:1, :]], 0)
    own_ref[0] = sums_ref[me, 0:1, :]
    turns = sorted(range(1, n_var), key=lambda d: -apart(d, n_var))
    for d in turns:
        var = lax.rem(va + d, n_var)
        slot = all_ref.at[va * n_samp + me]
        for o in far_first:
            for k in range(members):
                to(own_ref.at[0], slot, all_send, all_recv.at[va], group_of[o] * members + member_of[k], var)
    for o in far_first:
        each_member(o, lambda t: to(sums_ref.at[me], sums_ref.at[me], sum_send, sum_recv, t, va))

    def summed(var):
        z_ref[var] = jnp.sum(all_ref[pl.ds(var * n_samp, n_samp)], 0)

    arrived(sums_ref, n_samp - 1, sum_recv)
    for t in range(n_samp):
        all_ref[va * n_samp + t] = sums_ref[t, 0:1, :]
    summed(va)
    for d in turns[::-1]:
        var = lax.rem(va + n_var - d, n_var)
        arrived(all_ref, n_samp, all_recv.at[var])
        summed(var)
    every = jnp.broadcast_to(jnp.sum(z_ref[...], 0), (COLS, LANES))
    cc, cw, ww, rr, ri, ii = [
        jnp.sum(jnp.where(lane == row + COLS * k, every, 0.0), 1, keepdims=True) for k in range(6)
    ]

    delta = delta_ref[0]
    slope = ri / rr
    alpha0 = rr / (ri + delta * rr)
    norm1 = alpha0 * alpha0 * (ii - slope * ri)
    beta = norm1 / rr
    lead = alpha0 * slope + beta
    across = lead * lead * cc - 2.0 * lead * alpha0 * cw + alpha0 * alpha0 * ww
    alpha1 = norm1 / (across * (1.0 / m_total) + delta * (norm1 + beta * beta * rr))
    keep = alpha0 + alpha1 * lead
    less = alpha1 * alpha0
    sol_ref[...] = keep * rhs - less * image
    sol_out = pltpu.make_async_copy(sol_ref, sol_hbm, out_sem.at[0])
    sol_out.start()
    root = 1.0 / math.sqrt(n_total)
    keep_row = jnp.broadcast_to(keep[0:1, 0:1] * root, (1, LANES))
    less_row = jnp.broadcast_to(less[0:1, 0:1] * root, (1, LANES))
    for q in range(n_samp // n_core):
        at = q * n_core
        assoc_ref[q] = keep_row * c0_ref[at, 0:1, :] - less_row * sums_ref[at, 1:2, :]

    assoc_out = pltpu.make_async_copy(assoc_ref, assoc_hbm, out_sem.at[1])
    assoc_out.start()
    arrived(send1, n_samp - 1, rs_send.at[0])
    arrived(c0_ref, n_samp - 1, ag_send)
    arrived(part_ref, n_var - 1, var_sem.at[0])
    arrived(send2, n_samp - 1, rs_send.at[1])
    arrived(sums_ref, n_samp - 1, sum_send)
    arrived(all_ref, n_samp * (n_var - 1), all_send)
    sol_out.wait()
    assoc_out.wait()


def handed_on(sol_in, assoc_in, sol_out, assoc_out):
    sol_out[...] = sol_in[...]
    assoc_out[...] = assoc_in[...]


def per_device(places, n_var, genotypes, col_mean, inv_scale, targets, probes, delta):
    n_zl, n_x, n_y, n_core = places
    n_samp = math.prod(places)
    n_loc, m_loc = genotypes.shape
    groups, width = n_zl * n_x, n_y * LANES
    f32 = jnp.float32
    hbm = pl.BlockSpec(memory_space=pltpu.HBM)
    dma = pltpu.SemaphoreType.DMA
    sol, assoc = pl.pallas_call(
        functools.partial(kernel, places, n_var, n_loc * n_samp, m_loc * n_var),
        out_shape=(
            jax.ShapeDtypeStruct((COLS, n_loc), f32),
            jax.ShapeDtypeStruct((m_loc // LANES, 1, LANES), f32),
        ),
        in_specs=[hbm] * 6,
        out_specs=(hbm, hbm),
        scratch_shapes=[
            pltpu.VMEM((groups, n_loc, width), jnp.bfloat16),
            pltpu.VMEM((groups, 1, width), f32),
            pltpu.VMEM((groups, 1, width), f32),
            pltpu.VMEM((1, n_loc), f32),
            pltpu.VMEM((COLS - 1, n_loc), f32),
            pltpu.SMEM((1,), f32),
            pltpu.VMEM((COLS, n_loc), f32),
            pltpu.VMEM((m_loc // LANES, 1, LANES), f32),
            pltpu.VMEM((COLS, n_loc), f32),
            pltpu.VMEM((n_samp, COLS // n_core, LANES), f32),
            pltpu.VMEM((n_samp, COLS // n_core, LANES), f32),
            pltpu.VMEM((n_samp, COLS // n_core, LANES), f32),
            pltpu.VMEM((n_var, COLS, n_loc), f32),
            pltpu.VMEM((n_samp, COLS // n_core, LANES), f32),
            pltpu.VMEM((n_samp, COLS // n_core, LANES), f32),
            pltpu.VMEM((n_samp, 2, LANES), f32),
            pltpu.VMEM((1, 1, LANES), f32),
            pltpu.VMEM((n_var * n_samp, 1, LANES), f32),
            pltpu.VMEM((n_var, 1, LANES), f32),
            dma((groups,)),
            dma((5,)),
            dma((2,)),
            dma((2,)),
            dma((2,)),
            dma,
            dma((groups,)),
            dma((2,)),
            dma,
            dma,
            dma,
            dma((n_var,)),
        ],
        compiler_params=pltpu.CompilerParams(
            collective_id=0, has_side_effects=True, vmem_limit_bytes=60 * 1024 * 1024
        ),
    )(
        genotypes,
        col_mean.reshape(groups, 1, width),
        inv_scale.reshape(groups, 1, width),
        targets.reshape(1, n_loc),
        probes.T,
        delta,
    )
    sol, assoc = pl.pallas_call(
        handed_on,
        out_shape=(jax.ShapeDtypeStruct(sol.shape, f32), jax.ShapeDtypeStruct(assoc.shape, f32)),
        in_specs=[pl.BlockSpec(memory_space=pltpu.VMEM)] * 2,
        out_specs=(pl.BlockSpec(memory_space=pltpu.VMEM),) * 2,
    )(sol, assoc)
    return sol.T, assoc.reshape(m_loc)


def solution(mesh):
    places = PLACES
    if math.prod(places) != mesh.shape["samp"]:
        raise ValueError("samp size")
    placed = (P("samp", "var"), P("var"), P("var"), P("samp"), P("samp", None), P())
    return jax.shard_map(
        functools.partial(per_device, places, mesh.shape["var"]),
        mesh=mesh,
        in_specs=placed,
        out_specs=(P("samp", None), P("var")),
        check_vma=False,
    )
```

```python
import functools
import math

import jax
import jax.numpy as jnp
from jax import lax
from jax.experimental import pallas as pl
from jax.experimental.pallas import tpu as pltpu
from jax.sharding import PartitionSpec as P

MESH = pl.DeviceIdType.MESH
PLACES = (2, 4, 4, 2)
COLS = 8
LANES = 128
AHEAD = 3
HELD = 5


def apart(d, n):
    return min(d, n - d)


def three(v):
    high = v.astype(jnp.bfloat16).astype(jnp.float32)
    rest = v - high
    mid = rest.astype(jnp.bfloat16).astype(jnp.float32)
    low = rest - mid
    return jnp.concatenate([high, mid, low], 0).astype(jnp.bfloat16)


def folded(p):
    return p[0:COLS] + p[COLS : 2 * COLS] + p[2 * COLS : 3 * COLS]


def kernel(
    places, n_var, n_total, m_total,
    g_hbm, mean_hbm, inv_hbm, target_hbm, probe_hbm, delta_hbm,
    sol_ref, assoc_ref,
    g_ref, mean_ref, inv_ref, target_ref, probe_ref, delta_ref,
    rhs_ref, send1, recv1, c0_ref, part_ref, send2, recv2, sums_ref, own_ref, all_ref, z_ref,
    g_sem, in_sem, rs_send, rs_recv, ag_send, ag_recv, var_sem, sum_send, sum_recv, all_send, all_recv,
):
    n_zl, n_x, n_y, n_core = places
    n_samp = n_zl * n_x * n_y * n_core
    plane = n_x * n_y * n_core
    members = n_y * n_core
    half = COLS // n_core
    width = n_y * LANES
    me = lax.axis_index("samp")
    va = lax.axis_index("var")
    core = lax.rem(me, n_core)
    y = lax.rem(me // n_core, n_y)
    x = lax.rem(me // members, n_x)
    zl = me // plane
    mine = me // members
    offsets = [(dz, dx) for dz in range(n_zl) for dx in range(n_x)]
    near_first = sorted(offsets, key=lambda o: (o[0] + apart(o[1], n_x), o))
    far_first = near_first[::-1]
    group_of = {o: lax.rem(zl + o[0], n_zl) * n_x + lax.rem(x + o[1], n_x) for o in offsets}
    steps = sorted(((dy, dc) for dy in range(n_y) for dc in range(n_core)), key=lambda m: (-apart(m[0], n_y), -m[1]))
    steps.remove((0, 0))
    member_of = [lax.rem(y + dy, n_y) * n_core + lax.rem(core + dc, n_core) for dy, dc in steps + [(0, 0)]]

    def each_member(o, act):
        first = group_of[o] * members
        for k in range(members - (1 if o == (0, 0) else 0)):
            act(first + member_of[k])

    def to(src, dst, send, recv, samp, var):
        pltpu.make_async_remote_copy(
            src_ref=src, dst_ref=dst, send_sem=send, recv_sem=recv, device_id=(samp, var), device_id_type=MESH
        ).start()

    def arrived(ref, count, sem):
        some = ref.at[pl.ds(0, count)]
        pltpu.make_async_copy(some, some, sem).wait()

    def block(i, group):
        columns = pl.ds(pl.multiple_of(group * width, width), width)
        return pltpu.make_async_copy(g_hbm.at[:, columns], g_ref.at[group], g_sem.at[i])

    taken = [
        pltpu.make_async_copy(src, dst, in_sem.at[i])
        for i, (src, dst) in enumerate([
            (target_hbm, target_ref), (probe_hbm, probe_ref), (mean_hbm, mean_ref), (inv_hbm, inv_ref),
            (delta_hbm, delta_ref),
        ])
    ]
    for copy in taken:
        copy.start()
    for i in range(AHEAD):
        block(i, group_of[far_first[i]]).start()

    barrier = pltpu.get_barrier_semaphore()

    def greet(samp, var):
        pl.semaphore_signal(barrier, inc=1, device_id=(samp, var), device_id_type=MESH)

    others = [(o, k, o[0] + apart(o[1], n_x) + apart(m[0], n_y)) for o in offsets for k, m in enumerate(steps)]
    others += [(o, members - 1, o[0] + apart(o[1], n_x)) for o in offsets if o != (0, 0)]
    peers = [(hops, group_of[o] * members + member_of[k], va) for o, k, hops in others]
    peers += [(n_zl * apart(d, n_var), me, lax.rem(va + d, n_var)) for d in range(1, n_var)]
    for _, samp, var in sorted(peers, key=lambda p: -p[0]):
        greet(samp, var)

    for copy in taken:
        copy.wait()

    rhs_ref[0:1, :] = target_ref[...]
    rhs_ref[1:COLS, :] = probe_ref[...]
    rhs = rhs_ref[...]

    def reduced(vec, send, recv, sem, first, meanwhile):
        pieces = three(vec)
        total = jnp.sum(vec, 1, keepdims=True)

        def send_group(o):
            each_member(o, lambda t: to(send.at[t], recv.at[me], rs_send.at[sem], rs_recv.at[sem], t, va))

        for i, o in enumerate(far_first):
            group = group_of[o]
            if first:
                block(i, group).wait()
                if i + AHEAD < len(far_first):
                    block(i + AHEAD, group_of[far_first[i + AHEAD]]).start()
            p = folded(jnp.dot(pieces, g_ref[group], preferred_element_type=jnp.float32))
            p = p - total * mean_ref[group]
            held = min(HELD, len(far_first) - 1) if first else 1
            if first and i == held:
                pl.semaphore_wait(barrier, n_samp - 1 + n_var - 1)
            if i == held:
                for k in range(i):
                    send_group(far_first[k])
            elif i > held:
                send_group(far_first[i - 1])
            for ky in range(n_y):
                for kc in range(n_core):
                    send[group * members + ky * n_core + kc] = p[
                        kc * half : (kc + 1) * half, ky * LANES : (ky + 1) * LANES
                    ]
        send_group(far_first[-1])
        recv[me] = send[me]
        done = meanwhile()
        arrived(recv, n_samp - 1, rs_recv.at[sem])
        scale = inv_ref[mine, :, pl.ds(pl.multiple_of(y * LANES, LANES), LANES)]
        return jnp.sum(recv[...], 0) * scale, done

    share0, _ = reduced(rhs, send1, recv1, 0, True, lambda: None)
    c0_ref[me] = share0
    for o in far_first:
        each_member(o, lambda t: to(c0_ref.at[me], c0_ref.at[me], ag_send, ag_recv.at[mine], t, va))

    rows = None
    shift = None
    rings = sorted({o[0] + apart(o[1], n_x) for o in offsets})
    stages = [[o for o in near_first if o[0] + apart(o[1], n_x) == r] for r in rings]
    for stage in stages:
        for o in stage:
            arrived(c0_ref, members - (1 if o == (0, 0) else 0), ag_recv.at[group_of[o]])
        for o in stage:
            group = group_of[o]
            blocks = []
            for ky in range(n_y):
                blocks.append(
                    jnp.concatenate([c0_ref[group * members + ky * n_core + kc] for kc in range(n_core)], 0)
                )
            scaled = jnp.concatenate(blocks, 1) * inv_ref[group]
            off = jnp.sum(scaled * mean_ref[group], 1, keepdims=True)
            p = lax.dot_general(
                three(scaled), g_ref[group], (((1,), (1,)), ((), ())), preferred_element_type=jnp.float32
            )
            rows = p if rows is None else rows + p
            shift = off if shift is None else shift + off
    part_ref[va] = folded(rows) - shift
    for d in sorted(range(1, n_var), key=lambda d: -min(d, n_var - d)):
        to(part_ref.at[va], part_ref.at[va], var_sem.at[0], var_sem.at[1], me, lax.rem(va + d, n_var))
    arrived(part_ref, n_var - 1, var_sem.at[1])
    image = part_ref[0]
    for k in range(1, n_var):
        image = image + part_ref[k]
    image = image * (1.0 / m_total)

    row = lax.broadcasted_iota(jnp.int32, (COLS, LANES), 0)
    lane = lax.broadcasted_iota(jnp.int32, (COLS, LANES), 1)
    own = row // half == core

    def put(spread, k, q):
        return jnp.where(lane == row + COLS * k, jnp.sum(q, 1, keepdims=True), spread)

    def by_column(a):
        return jnp.where(own, jnp.concatenate([a] * n_core, 0), 0.0)

    def known():
        spread = put(jnp.zeros((COLS, LANES), jnp.float32), 0, by_column(share0 * share0))
        for k, (a, b) in enumerate([(rhs, rhs), (rhs, image), (image, image)]):
            spread = put(spread, 3 + k, a * b * (1.0 / n_var))
        return spread

    share1, spread = reduced(image, send2, recv2, 1, False, known)
    spread = put(spread, 1, by_column(share0 * share1))
    spread = put(spread, 2, by_column(share1 * share1))
    sums_ref[me] = jnp.concatenate([jnp.sum(spread, 0, keepdims=True), share1[0:1, :]], 0)
    own_ref[0] = sums_ref[me, 0:1, :]
    turns = sorted(range(1, n_var), key=lambda d: -apart(d, n_var))
    for d in turns:
        var = lax.rem(va + d, n_var)
        slot = all_ref.at[va * n_samp + me]
        for o in far_first:
            for k in range(members):
                to(own_ref.at[0], slot, all_send, all_recv.at[va], group_of[o] * members + member_of[k], var)
    for o in far_first:
        each_member(o, lambda t: to(sums_ref.at[me], sums_ref.at[me], sum_send, sum_recv, t, va))

    def summed(var):
        z_ref[var] = jnp.sum(all_ref[pl.ds(var * n_samp, n_samp)], 0)

    arrived(sums_ref, n_samp - 1, sum_recv)
    for t in range(n_samp):
        all_ref[va * n_samp + t] = sums_ref[t, 0:1, :]
    summed(va)
    for d in turns[::-1]:
        var = lax.rem(va + n_var - d, n_var)
        arrived(all_ref, n_samp, all_recv.at[var])
        summed(var)
    every = jnp.broadcast_to(jnp.sum(z_ref[...], 0), (COLS, LANES))
    cc, cw, ww, rr, ri, ii = [
        jnp.sum(jnp.where(lane == row + COLS * k, every, 0.0), 1, keepdims=True) for k in range(6)
    ]

    delta = delta_ref[0]
    slope = ri / rr
    alpha0 = rr / (ri + delta * rr)
    norm1 = alpha0 * alpha0 * (ii - slope * ri)
    beta = norm1 / rr
    lead = alpha0 * slope + beta
    across = lead * lead * cc - 2.0 * lead * alpha0 * cw + alpha0 * alpha0 * ww
    alpha1 = norm1 / (across * (1.0 / m_total) + delta * (norm1 + beta * beta * rr))
    keep = alpha0 + alpha1 * lead
    less = alpha1 * alpha0
    sol_ref[...] = keep * rhs - less * image
    root = 1.0 / math.sqrt(n_total)
    keep_row = jnp.broadcast_to(keep[0:1, 0:1] * root, (1, LANES))
    less_row = jnp.broadcast_to(less[0:1, 0:1] * root, (1, LANES))
    for q in range(n_samp // n_core):
        at = q * n_core
        assoc_ref[q] = keep_row * c0_ref[at, 0:1, :] - less_row * sums_ref[at, 1:2, :]

    arrived(send1, n_samp - 1, rs_send.at[0])
    arrived(c0_ref, n_samp - 1, ag_send)
    arrived(part_ref, n_var - 1, var_sem.at[0])
    arrived(send2, n_samp - 1, rs_send.at[1])
    arrived(sums_ref, n_samp - 1, sum_send)
    arrived(all_ref, n_samp * (n_var - 1), all_send)


def handed_on(sol_in, assoc_in, sol_out, assoc_out):
    sol_out[...] = sol_in[...]
    assoc_out[...] = assoc_in[...]


def per_device(places, n_var, genotypes, col_mean, inv_scale, targets, probes, delta):
    n_zl, n_x, n_y, n_core = places
    n_samp = math.prod(places)
    n_loc, m_loc = genotypes.shape
    groups, width = n_zl * n_x, n_y * LANES
    f32 = jnp.float32
    hbm = pl.BlockSpec(memory_space=pltpu.HBM)
    vmem = pl.BlockSpec(memory_space=pltpu.VMEM)
    dma = pltpu.SemaphoreType.DMA
    sol, assoc = pl.pallas_call(
        functools.partial(kernel, places, n_var, n_loc * n_samp, m_loc * n_var),
        out_shape=(
            pltpu.VMEM((COLS, n_loc), f32),
            pltpu.VMEM((m_loc // LANES, 1, LANES), f32),
        ),
        in_specs=[hbm] * 6,
        out_specs=(vmem, vmem),
        scratch_shapes=[
            pltpu.VMEM((groups, n_loc, width), jnp.bfloat16),
            pltpu.VMEM((groups, 1, width), f32),
            pltpu.VMEM((groups, 1, width), f32),
            pltpu.VMEM((1, n_loc), f32),
            pltpu.VMEM((COLS - 1, n_loc), f32),
            pltpu.SMEM((1,), f32),
            pltpu.VMEM((COLS, n_loc), f32),
            pltpu.VMEM((n_samp, COLS // n_core, LANES), f32),
            pltpu.VMEM((n_samp, COLS // n_core, LANES), f32),
            pltpu.VMEM((n_samp, COLS // n_core, LANES), f32),
            pltpu.VMEM((n_var, COLS, n_loc), f32),
            pltpu.VMEM((n_samp, COLS // n_core, LANES), f32),
            pltpu.VMEM((n_samp, COLS // n_core, LANES), f32),
            pltpu.VMEM((n_samp, 2, LANES), f32),
            pltpu.VMEM((1, 1, LANES), f32),
            pltpu.VMEM((n_var * n_samp, 1, LANES), f32),
            pltpu.VMEM((n_var, 1, LANES), f32),
            dma((groups,)),
            dma((5,)),
            dma((2,)),
            dma((2,)),
            dma,
            dma((groups,)),
            dma((2,)),
            dma,
            dma,
            dma,
            dma((n_var,)),
        ],
        compiler_params=pltpu.CompilerParams(
            collective_id=0, has_side_effects=True, vmem_limit_bytes=60 * 1024 * 1024
        ),
    )(
        genotypes,
        col_mean.reshape(groups, 1, width),
        inv_scale.reshape(groups, 1, width),
        targets.reshape(1, n_loc),
        probes.T,
        delta,
    )
    sol, assoc = pl.pallas_call(
        handed_on,
        out_shape=(jax.ShapeDtypeStruct(sol.shape, f32), jax.ShapeDtypeStruct(assoc.shape, f32)),
        in_specs=[pl.BlockSpec(memory_space=pltpu.VMEM)] * 2,
        out_specs=(pl.BlockSpec(memory_space=pltpu.VMEM),) * 2,
    )(pltpu.with_memory_space_constraint(sol, pltpu.VMEM), pltpu.with_memory_space_constraint(assoc, pltpu.VMEM))
    return sol.T, assoc.reshape(m_loc)


def solution(mesh):
    places = PLACES
    if math.prod(places) != mesh.shape["samp"]:
        raise ValueError("samp size")
    placed = (P("samp", "var"), P("var"), P("var"), P("samp"), P("samp", None), P())
    return jax.shard_map(
        functools.partial(per_device, places, mesh.shape["var"]),
        mesh=mesh,
        in_specs=placed,
        out_specs=(P("samp", None), P("var")),
        check_vma=False,
    )
```

```python
import functools
import math

import jax
import jax.numpy as jnp
from jax import lax
from jax.experimental import pallas as pl
from jax.experimental.pallas import tpu as pltpu
from jax.sharding import PartitionSpec as P

MESH = pl.DeviceIdType.MESH
PLACES = (2, 4, 4, 2)
COLS = 8
LANES = 128
CUTS = (1, 4, 7)
AHEAD = 3
HELD = 5


def apart(d, n):
    return min(d, n - d)


def two(v):
    high = v.astype(jnp.bfloat16).astype(jnp.float32)
    low = (v - high).astype(jnp.bfloat16).astype(jnp.float32)
    return jnp.concatenate([high, low], 0).astype(jnp.bfloat16), high + low


def folded(p):
    return p[0:COLS] + p[COLS : 2 * COLS]


def kernel(
    places, n_var, n_total, m_total,
    g_hbm, mean_hbm, inv_hbm, target_hbm, probe_hbm, delta_hbm,
    sol_ref, assoc_ref,
    g_ref, mean_ref, inv_ref, target_ref, probe_ref, delta_ref,
    rhs_ref, send1, recv1, c0_ref, part_ref, send2, recv2, sums_ref, own_ref, all_ref, z_ref,
    g_sem, in_sem, rs_send, rs_recv, ag_send, ag_recv, var_sem, sum_send, sum_recv, all_send, all_recv,
):
    n_zl, n_x, n_y, n_core = places
    n_samp = n_zl * n_x * n_y * n_core
    plane = n_x * n_y * n_core
    members = n_y * n_core
    half = COLS // n_core
    width = n_y * LANES
    me = lax.axis_index("samp")
    va = lax.axis_index("var")
    core = lax.rem(me, n_core)
    y = lax.rem(me // n_core, n_y)
    x = lax.rem(me // members, n_x)
    zl = me // plane
    mine = me // members
    offsets = [(dz, dx) for dz in range(n_zl) for dx in range(n_x)]
    near_first = sorted(offsets, key=lambda o: (o[0] + apart(o[1], n_x), o))
    far_first = near_first[::-1]
    group_of = {o: lax.rem(zl + o[0], n_zl) * n_x + lax.rem(x + o[1], n_x) for o in offsets}
    steps = sorted(((dy, dc) for dy in range(n_y) for dc in range(n_core)), key=lambda m: (-apart(m[0], n_y), -m[1]))
    steps.remove((0, 0))
    member_of = [lax.rem(y + dy, n_y) * n_core + lax.rem(core + dc, n_core) for dy, dc in steps + [(0, 0)]]

    def each_member(o, act):
        first = group_of[o] * members
        for k in range(members - (1 if o == (0, 0) else 0)):
            act(first + member_of[k])

    def to(src, dst, send, recv, samp, var):
        pltpu.make_async_remote_copy(
            src_ref=src, dst_ref=dst, send_sem=send, recv_sem=recv, device_id=(samp, var), device_id_type=MESH
        ).start()

    def arrived(ref, count, sem):
        some = ref.at[pl.ds(0, count)]
        pltpu.make_async_copy(some, some, sem).wait()

    def block(i, group):
        columns = pl.ds(pl.multiple_of(group * width, width), width)
        return pltpu.make_async_copy(g_hbm.at[:, columns], g_ref.at[group], g_sem.at[i])

    taken = [
        pltpu.make_async_copy(src, dst, in_sem.at[i])
        for i, (src, dst) in enumerate([
            (target_hbm, target_ref), (probe_hbm, probe_ref), (mean_hbm, mean_ref), (inv_hbm, inv_ref),
            (delta_hbm, delta_ref),
        ])
    ]
    for copy in taken:
        copy.start()
    for i in range(AHEAD):
        block(i, group_of[far_first[i]]).start()

    barrier = pltpu.get_barrier_semaphore()

    def greet(samp, var):
        pl.semaphore_signal(barrier, inc=1, device_id=(samp, var), device_id_type=MESH)

    others = [(o, k, o[0] + apart(o[1], n_x) + apart(m[0], n_y)) for o in offsets for k, m in enumerate(steps)]
    others += [(o, members - 1, o[0] + apart(o[1], n_x)) for o in offsets if o != (0, 0)]
    peers = [(hops, group_of[o] * members + member_of[k], va) for o, k, hops in others]
    peers += [(n_zl * apart(d, n_var), me, lax.rem(va + d, n_var)) for d in range(1, n_var)]
    for _, samp, var in sorted(peers, key=lambda p: -p[0]):
        greet(samp, var)

    for copy in taken:
        copy.wait()

    rhs_ref[0:1, :] = target_ref[...]
    rhs_ref[1:COLS, :] = probe_ref[...]
    rhs = rhs_ref[...]

    def reduced(vec, send, recv, sem, first, meanwhile):
        pieces, whole = two(vec)
        total = jnp.sum(whole, 1, keepdims=True)

        def send_group(o):
            each_member(o, lambda t: to(send.at[t], recv.at[me], rs_send.at[sem], rs_recv.at[sem], t, va))

        def product(o):
            p = folded(jnp.dot(pieces, g_ref[group_of[o]], preferred_element_type=jnp.float32))
            return p - total * mean_ref[group_of[o]]

        def store(o, p):
            for ky in range(n_y):
                for kc in range(n_core):
                    send[group_of[o] * members + ky * n_core + kc] = p[
                        kc * half : (kc + 1) * half, ky * LANES : (ky + 1) * LANES
                    ]

        held = min(HELD, len(far_first) - 1)
        if first:
            for i, o in enumerate(far_first):
                block(i, group_of[o]).wait()
                if i + AHEAD < len(far_first):
                    block(i + AHEAD, group_of[far_first[i + AHEAD]]).start()
                p = product(o)
                if i == held:
                    pl.semaphore_wait(barrier, n_samp - 1 + n_var - 1)
                    for k in range(i):
                        send_group(far_first[k])
                elif i > held:
                    send_group(far_first[i - 1])
                store(o, p)
            send_group(far_first[-1])
        else:
            cuts = [c for c in CUTS if c < len(far_first)] + [len(far_first)]
            for lo, hi in zip([0] + cuts, cuts):
                stage = far_first[lo:hi]
                done = [product(o) for o in stage]
                for o, p in zip(stage, done):
                    store(o, p)
                for o in stage:
                    send_group(o)
        recv[me] = send[me]
        done = meanwhile()
        arrived(recv, n_samp - 1, rs_recv.at[sem])
        scale = inv_ref[mine, :, pl.ds(pl.multiple_of(y * LANES, LANES), LANES)]
        return jnp.sum(recv[...], 0) * scale, done

    share0, _ = reduced(rhs, send1, recv1, 0, True, lambda: None)
    c0_ref[me] = share0
    for o in far_first:
        each_member(o, lambda t: to(c0_ref.at[me], c0_ref.at[me], ag_send, ag_recv.at[mine], t, va))

    rows = None
    shift = None
    rings = sorted({o[0] + apart(o[1], n_x) for o in offsets})
    stages = [[o for o in near_first if o[0] + apart(o[1], n_x) == r] for r in rings]
    for stage in stages:
        for o in stage:
            arrived(c0_ref, members - (1 if o == (0, 0) else 0), ag_recv.at[group_of[o]])
        for o in stage:
            group = group_of[o]
            blocks = []
            for ky in range(n_y):
                blocks.append(
                    jnp.concatenate([c0_ref[group * members + ky * n_core + kc] for kc in range(n_core)], 0)
                )
            scaled = jnp.concatenate(blocks, 1) * inv_ref[group]
            pieces, whole = two(scaled)
            off = jnp.sum(whole * mean_ref[group], 1, keepdims=True)
            p = lax.dot_general(
                pieces, g_ref[group], (((1,), (1,)), ((), ())), preferred_element_type=jnp.float32
            )
            rows = p if rows is None else rows + p
            shift = off if shift is None else shift + off
    part_ref[va] = folded(rows) - shift
    for d in sorted(range(1, n_var), key=lambda d: -min(d, n_var - d)):
        to(part_ref.at[va], part_ref.at[va], var_sem.at[0], var_sem.at[1], me, lax.rem(va + d, n_var))
    arrived(part_ref, n_var - 1, var_sem.at[1])
    image = part_ref[0]
    for k in range(1, n_var):
        image = image + part_ref[k]
    image = image * (1.0 / m_total)

    row = lax.broadcasted_iota(jnp.int32, (COLS, LANES), 0)
    lane = lax.broadcasted_iota(jnp.int32, (COLS, LANES), 1)
    own = row // half == core

    def put(spread, k, q):
        return jnp.where(lane == row + COLS * k, jnp.sum(q, 1, keepdims=True), spread)

    def by_column(a):
        return jnp.where(own, jnp.concatenate([a] * n_core, 0), 0.0)

    def known():
        spread = put(jnp.zeros((COLS, LANES), jnp.float32), 0, by_column(share0 * share0))
        for k, (a, b) in enumerate([(rhs, rhs), (rhs, image), (image, image)]):
            spread = put(spread, 3 + k, a * b * (1.0 / n_var))
        return spread

    share1, spread = reduced(image, send2, recv2, 1, False, known)
    spread = put(spread, 1, by_column(share0 * share1))
    spread = put(spread, 2, by_column(share1 * share1))
    sums_ref[me] = jnp.concatenate([jnp.sum(spread, 0, keepdims=True), share1[0:1, :]], 0)
    own_ref[0] = sums_ref[me, 0:1, :]
    turns = sorted(range(1, n_var), key=lambda d: -apart(d, n_var))
    slot = all_ref.at[va * n_samp + me]
    along = {d: lax.rem(va + n_var + (1 - 2 * zl) * d, n_var) for d in turns}
    every_one = []
    for o in offsets:
        for k, m in enumerate(steps + [(0, 0)]):
            flat = apart(o[1], n_x) + apart(m[0], n_y)
            every_one += [(apart(d * n_zl + o[0], n_var * n_zl) + flat, o, k, d) for d in range(n_var)]
    every_one.remove((0, (0, 0), members - 1, 0))
    for _, o, k, d in sorted(every_one, key=lambda e: -e[0]):
        samp = group_of[o] * members + member_of[k]
        if d:
            to(own_ref.at[0], slot, all_send, all_recv.at[va], samp, along[d])
        else:
            to(sums_ref.at[me], sums_ref.at[me], sum_send, sum_recv, samp, va)

    def summed(var):
        z_ref[var] = jnp.sum(all_ref[pl.ds(var * n_samp, n_samp)], 0)

    arrived(sums_ref, n_samp - 1, sum_recv)
    for t in range(n_samp):
        all_ref[va * n_samp + t] = sums_ref[t, 0:1, :]
    summed(va)
    for d in turns[::-1]:
        var = lax.rem(va + n_var - d, n_var)
        arrived(all_ref, n_samp, all_recv.at[var])
        summed(var)
    every = jnp.broadcast_to(jnp.sum(z_ref[...], 0), (COLS, LANES))
    cc, cw, ww, rr, ri, ii = [
        jnp.sum(jnp.where(lane == row + COLS * k, every, 0.0), 1, keepdims=True) for k in range(6)
    ]

    delta = delta_ref[0]
    slope = ri / rr
    alpha0 = rr / (ri + delta * rr)
    norm1 = alpha0 * alpha0 * (ii - slope * ri)
    beta = norm1 / rr
    lead = alpha0 * slope + beta
    across = lead * lead * cc - 2.0 * lead * alpha0 * cw + alpha0 * alpha0 * ww
    alpha1 = norm1 / (across * (1.0 / m_total) + delta * (norm1 + beta * beta * rr))
    keep = alpha0 + alpha1 * lead
    less = alpha1 * alpha0
    sol_ref[...] = keep * rhs - less * image
    root = 1.0 / math.sqrt(n_total)
    keep_row = jnp.broadcast_to(keep[0:1, 0:1] * root, (1, LANES))
    less_row = jnp.broadcast_to(less[0:1, 0:1] * root, (1, LANES))
    for q in range(n_samp // n_core):
        at = q * n_core
        assoc_ref[q] = keep_row * c0_ref[at, 0:1, :] - less_row * sums_ref[at, 1:2, :]

    arrived(send1, n_samp - 1, rs_send.at[0])
    arrived(c0_ref, n_samp - 1, ag_send)
    arrived(part_ref, n_var - 1, var_sem.at[0])
    arrived(send2, n_samp - 1, rs_send.at[1])
    arrived(sums_ref, n_samp - 1, sum_send)
    arrived(all_ref, n_samp * (n_var - 1), all_send)


def handed_on(sol_in, assoc_in, sol_out, assoc_out):
    sol_out[...] = sol_in[...]
    assoc_out[...] = assoc_in[...]


def per_device(places, n_var, genotypes, col_mean, inv_scale, targets, probes, delta):
    n_zl, n_x, n_y, n_core = places
    n_samp = math.prod(places)
    n_loc, m_loc = genotypes.shape
    groups, width = n_zl * n_x, n_y * LANES
    f32 = jnp.float32
    hbm = pl.BlockSpec(memory_space=pltpu.HBM)
    vmem = pl.BlockSpec(memory_space=pltpu.VMEM)
    dma = pltpu.SemaphoreType.DMA
    sol, assoc = pl.pallas_call(
        functools.partial(kernel, places, n_var, n_loc * n_samp, m_loc * n_var),
        out_shape=(
            pltpu.VMEM((COLS, n_loc), f32),
            pltpu.VMEM((m_loc // LANES, 1, LANES), f32),
        ),
        in_specs=[hbm] * 6,
        out_specs=(vmem, vmem),
        scratch_shapes=[
            pltpu.VMEM((groups, n_loc, width), jnp.bfloat16),
            pltpu.VMEM((groups, 1, width), f32),
            pltpu.VMEM((groups, 1, width), f32),
            pltpu.VMEM((1, n_loc), f32),
            pltpu.VMEM((COLS - 1, n_loc), f32),
            pltpu.SMEM((1,), f32),
            pltpu.VMEM((COLS, n_loc), f32),
            pltpu.VMEM((n_samp, COLS // n_core, LANES), f32),
            pltpu.VMEM((n_samp, COLS // n_core, LANES), f32),
            pltpu.VMEM((n_samp, COLS // n_core, LANES), f32),
            pltpu.VMEM((n_var, COLS, n_loc), f32),
            pltpu.VMEM((n_samp, COLS // n_core, LANES), f32),
            pltpu.VMEM((n_samp, COLS // n_core, LANES), f32),
            pltpu.VMEM((n_samp, 2, LANES), f32),
            pltpu.VMEM((1, 1, LANES), f32),
            pltpu.VMEM((n_var * n_samp, 1, LANES), f32),
            pltpu.VMEM((n_var, 1, LANES), f32),
            dma((groups,)),
            dma((5,)),
            dma((2,)),
            dma((2,)),
            dma,
            dma((groups,)),
            dma((2,)),
            dma,
            dma,
            dma,
            dma((n_var,)),
        ],
        compiler_params=pltpu.CompilerParams(
            collective_id=0, has_side_effects=True, vmem_limit_bytes=60 * 1024 * 1024
        ),
    )(
        genotypes,
        col_mean.reshape(groups, 1, width),
        inv_scale.reshape(groups, 1, width),
        targets.reshape(1, n_loc),
        probes.T,
        delta,
    )
    sol, assoc = pl.pallas_call(
        handed_on,
        out_shape=(jax.ShapeDtypeStruct(sol.shape, f32), jax.ShapeDtypeStruct(assoc.shape, f32)),
        in_specs=[pl.BlockSpec(memory_space=pltpu.VMEM)] * 2,
        out_specs=(pl.BlockSpec(memory_space=pltpu.VMEM),) * 2,
    )(pltpu.with_memory_space_constraint(sol, pltpu.VMEM), pltpu.with_memory_space_constraint(assoc, pltpu.VMEM))
    return sol.T, assoc.reshape(m_loc)


def solution(mesh):
    places = PLACES
    if math.prod(places) != mesh.shape["samp"]:
        raise ValueError("samp size")
    placed = (P("samp", "var"), P("var"), P("var"), P("samp"), P("samp", None), P())
    return jax.shard_map(
        functools.partial(per_device, places, mesh.shape["var"]),
        mesh=mesh,
        in_specs=placed,
        out_specs=(P("samp", None), P("var")),
        check_vma=False,
    )
```
